32 devices in a mesh: slide: 4 (over x, core), rows: 8 (over z, y).
Axes of the slice: x: 2, y: 2, z: 4, core: 2. Of those that a mesh axis runs over, the one named last changes fastest.
Arguments:
- features: bfloat16 [4, 192, 256, 128], P('slide', None, 'rows'), may hold values from -6 to 6
- depth_kernel: float32 [192, 49], replicated, may hold values from -0.875 to 0.875
- depth_bias: float32 [192], replicated, may hold values from -4 to 4
- norm_gain: float32 [192], replicated, may hold values from 0.1 to 1.9
- norm_bias: float32 [192], replicated, may hold values from -3 to 3
- up_weight: bfloat16 [192, 768], replicated, may hold values from -0.4375 to 0.4375
- up_bias: float32 [768], replicated, may hold values from -3 to 3
- down_weight: bfloat16 [768, 192], replicated, may hold values from -0.21875 to 0.21875
- down_bias: float32 [192], replicated, may hold values from -4 to 4
- layer_scale: float32 [192], replicated, may hold values from 0.2 to 1
- tissue: int32 [4, 8, 4], P('slide', 'rows'), may hold values 0 or 1
- aggregator_order: int32 [4, 32], P('slide'), may hold values from 0 to 31, each once within a row
- tile_cotangent: bfloat16 [4, 32, 192], P('slide', 'rows'), may hold values from -6 to 6
Outputs:
- embedding: float32 [4, 32, 192], P('slide', 'rows')
- input_grad: bfloat16 [4, 192, 256, 128], P('slide', None, 'rows')
- grad_up: float32 [192, 768], replicated
- grad_down: float32 [768, 192], replicated
- grad_kernel: float32 [192, 49], replicated
The draws below stay inside these ranges and needn't reach their ends.
Inputs may be any that keep to these rules, and one draw needn't show every extreme that they name: `aggregator_order`: each slide's row is a permutation of the 32 positions.
All inputs are finite; a program needn't handle non-finite values. No bound on the sum of `tissue` on one device may be relied on, other than what follows from the above.
Results may differ from the reference program's by a relative error of at most 0.0064.
Values may be sent and summed in bfloat16 or wider, within the bound.
A program may use at most 128 MiB of HBM per device.

```python
import math
import jax
import jax.numpy as jnp
from jax import lax

C = 192
HID = 768
TILE = 32
WIDTH = 128
SLIDES = 4
HEIGHT = 256
TILES_DEV = 4
TILES = 32


def plant(entries, stream_key, least, top_value):
    place = [jax.random.randint(jax.random.fold_in(stream_key, axis), (), 0, length) for axis, length in enumerate(entries.shape)]
    longest = entries.shape.index(max(entries.shape))
    beside = place[:longest] + [(place[longest] + 1) % entries.shape[longest]] + place[longest + 1:]
    return entries.at[tuple(place)].set(least).at[tuple(beside)].set(top_value)


def steps_of(own_key, shape, split, least, high):
    gain = 1.0
    for dim, parts in split:
        heights = jax.random.uniform(jax.random.fold_in(jax.random.fold_in(own_key, 6), dim), (parts,), jnp.float32, least / len(split), high / len(split))
        gain = gain * jnp.repeat(jnp.exp(heights), shape[dim] // parts).reshape((-1,) + (1,) * (len(shape) - 1 - dim))
    return gain


def normal_values(stream_key, dims, spread, limit, shards=(), held_as=jnp.bfloat16):
    result = spread * jax.random.normal(stream_key, dims, jnp.float32)
    if shards:
        result = result * steps_of(stream_key, dims, shards, -0.22, 0.18)
    return jnp.clip(result, -limit, limit).astype(held_as)


def setup_inputs(seed: int = 0) -> dict:
    key_list = jax.random.split(jax.random.key(seed), 14)
    return {
        "features": normal_values(key_list[0], (SLIDES, C, HEIGHT, WIDTH), 1.0, 6.0, ((0, 4), (2, 8))),
        "depth_kernel": normal_values(key_list[1], (C, 49), 49 ** -0.5, 0.875, (), jnp.float32),
        "depth_bias": normal_values(key_list[2], (C,), 1.0, 4.0, (), jnp.float32),
        "norm_gain": jnp.clip(1.0 + 0.18 * jax.random.normal(key_list[3], (C,), jnp.float32), 0.1, 1.9),
        "norm_bias": normal_values(key_list[4], (C,), 0.5, 3.0, (), jnp.float32),
        "up_weight": normal_values(key_list[5], (C, HID), C ** -0.5, 0.4375),
        "up_bias": normal_values(key_list[6], (HID,), 0.5, 3.0, (), jnp.float32),
        "down_weight": normal_values(key_list[7], (HID, C), HID ** -0.5, 0.21875),
        "down_bias": normal_values(key_list[8], (C,), 1.0, 4.0, (), jnp.float32),
        "layer_scale": jnp.clip(jnp.exp(jax.random.uniform(key_list[9], (C,), jnp.float32, math.log(0.2), math.log(1.0))), 0.2, 1.0),
        "tissue": plant((jax.random.randint(key_list[10], (SLIDES, HEIGHT // TILE, TILES_DEV), 0, 3) < 2).astype(jnp.int32), jax.random.fold_in(key_list[10], 1), 0, 1),
        "aggregator_order": jax.vmap(lambda own: jax.random.permutation(own, TILES))(jax.random.split(key_list[11], SLIDES)).reshape((SLIDES, TILES)).astype(jnp.int32),
        "tile_cotangent": normal_values(key_list[12], (SLIDES, TILES, C), 1.0, 6.0, ((0, 4), (1, 8))),
    }


def depthwise(source, kernel, height, across, mirrored):
    channels = source.shape[0]
    total = jnp.zeros((channels, height, across), jnp.float32)
    for position in range(49):
        row_start = position // 7
        col_start = position % 7
        if mirrored:
            row_start = 6 - row_start
            col_start = 6 - col_start
        window = lax.slice(source, (0, row_start, col_start), (channels, row_start + height, col_start + across))
        total = total + kernel[:, position][:, None, None] * window.astype(jnp.float32)
    return total

def gelu_exact(values):
    return 0.5 * values * (1.0 + jax.scipy.special.erf(values * 0.7071067811865476))

def gelu_slope(values):
    cumulative = 0.5 * (1.0 + jax.scipy.special.erf(values * 0.7071067811865476))
    density = jnp.exp(-0.5 * values * values) * 0.3989422804014327
    return cumulative + values * density

def block_pass(conv_flat, image_flat, pixel_mask, pixel_cotangent, norm_gain, norm_bias, up_weight, up_bias, down_weight, down_bias, layer_scale):
    average = lax.optimization_barrier(jnp.mean(conv_flat, axis=0, keepdims=True))
    centered = conv_flat - average
    variance = lax.optimization_barrier(jnp.mean(centered * centered, axis=0, keepdims=True))
    reciprocal = lax.rsqrt(variance + 1e-06)
    standard = centered * reciprocal
    normed = (standard * norm_gain[:, None] + norm_bias[:, None]).astype(jnp.bfloat16)
    activation_in = jnp.dot(up_weight.T, normed, preferred_element_type=jnp.float32) + up_bias[:, None]
    hidden = gelu_exact(activation_in).astype(jnp.bfloat16)
    branch = jnp.dot(down_weight.T, hidden, preferred_element_type=jnp.float32) + down_bias[:, None]
    scaled_mask = pixel_mask[None, :] * layer_scale[:, None]
    output = image_flat.astype(jnp.float32) + scaled_mask * branch
    grad_branch = (scaled_mask * pixel_cotangent).astype(jnp.bfloat16)
    grad_hidden = jnp.dot(down_weight, grad_branch, preferred_element_type=jnp.float32)
    grad_activation = (grad_hidden * gelu_slope(activation_in)).astype(jnp.bfloat16)
    grad_normed = jnp.dot(up_weight, grad_activation, preferred_element_type=jnp.float32)
    grad_standard = grad_normed * norm_gain[:, None]
    grad_conv = reciprocal * (grad_standard - lax.optimization_barrier(jnp.mean(grad_standard, axis=0, keepdims=True)) - standard * lax.optimization_barrier(jnp.mean(grad_standard * standard, axis=0, keepdims=True)))
    grad_conv = grad_conv.astype(jnp.bfloat16)
    up_term = jnp.dot(normed, grad_activation.T, preferred_element_type=jnp.float32)
    down_term = jnp.dot(grad_branch, hidden.T, preferred_element_type=jnp.float32)
    return (output, grad_conv, up_term, down_term)

def reference(features, depth_kernel, depth_bias, norm_gain, norm_bias, up_weight, up_bias, down_weight, down_bias, layer_scale, tissue, aggregator_order, tile_cotangent):
    loss_norm = 1.0 / math.sqrt(SLIDES * HEIGHT * WIDTH)
    tile_rows = HEIGHT // TILE
    block_pixels = TILE * WIDTH

    def slide_pass(inputs):
        pixels_in, tissue_map, order, cotangent = inputs
        extended = jnp.pad(pixels_in, ((0, 0), (3, 3), (3, 3)))
        convolved = depthwise(extended, depth_kernel, HEIGHT, WIDTH, False) + depth_bias[:, None, None]
        wanted = jnp.take(cotangent, order.astype(jnp.int32), axis=0).astype(jnp.float32)
        wanted = wanted.reshape(tile_rows, TILES_DEV, C)
        masks = tissue_map.astype(jnp.float32)
        conv_rows = convolved.reshape(C, tile_rows, block_pixels).transpose(1, 0, 2)
        image_rows = pixels_in.reshape(C, tile_rows, block_pixels).transpose(1, 0, 2)

        def row_pass(carry, row_inputs):
            conv_flat, image_flat, mask_row, cotangent_row = row_inputs
            pixel_mask = jnp.broadcast_to(mask_row[None, :, None], (TILE, TILES_DEV, TILE)).reshape(block_pixels)
            pixel_cotangent = jnp.broadcast_to(cotangent_row.T[:, None, :, None], (C, TILE, TILES_DEV, TILE)).reshape(C, block_pixels)
            output, grad_conv, up_term, down_term = block_pass(conv_flat, image_flat, pixel_mask, pixel_cotangent, norm_gain, norm_bias, up_weight, up_bias, down_weight, down_bias, layer_scale)
            embedded = lax.optimization_barrier(jnp.mean(output.reshape(C, TILE, TILES_DEV, TILE), axis=(1, 3))).T
            return ((carry[0] + up_term, carry[1] + down_term), (embedded, grad_conv, pixel_cotangent))
        start = (jnp.zeros((C, HID), jnp.float32), jnp.zeros((C, HID), jnp.float32))
        sums, stacked = lax.scan(row_pass, start, (conv_rows, image_rows, masks, wanted))
        embedded, grad_convs, cotangents = stacked
        grad_image = grad_convs.transpose(1, 0, 2).reshape(C, HEIGHT, WIDTH)
        cotangent_image = cotangents.transpose(1, 0, 2).reshape(C, HEIGHT, WIDTH)
        grad_extended = jnp.pad(grad_image, ((0, 0), (3, 3), (3, 3)))
        input_grad = (cotangent_image + depthwise(grad_extended, depth_kernel, HEIGHT, WIDTH, True)).astype(jnp.bfloat16)
        kernel_cols = []
        for position in range(49):
            row_start = position // 7
            col_start = position % 7
            window = lax.slice(extended, (0, row_start, col_start), (C, row_start + HEIGHT, col_start + WIDTH))
            kernel_cols.append(lax.optimization_barrier(jnp.sum(grad_image.astype(jnp.float32) * window.astype(jnp.float32), axis=(1, 2))))
        kernel_term = jnp.stack(kernel_cols, axis=1)
        return (embedded.reshape(TILES, C), input_grad, sums[0], sums[1], kernel_term)
    results = lax.map(slide_pass, (features, tissue, aggregator_order, tile_cotangent))
    grad_up = lax.optimization_barrier(jnp.sum(results[2], axis=0)) * loss_norm
    grad_down = lax.optimization_barrier(jnp.sum(results[3], axis=0)).T * loss_norm
    grad_kernel = lax.optimization_barrier(jnp.sum(results[4], axis=0)) * loss_norm
    return (results[0], results[1], grad_up, grad_down, grad_kernel)
```

```python
import functools
import math

import jax
import jax.numpy as jnp
from jax import lax
from jax.experimental import pallas as pl
from jax.experimental.pallas import tpu as pltpu
from jax.sharding import PartitionSpec as P

TILE = 32
ROWS = 4
HALF = 16
TAPS = 7
PAD = 3
EDGE = 4
LANES = 128
MESH = pl.DeviceIdType.MESH
VMEM = pl.BlockSpec(memory_space=pltpu.VMEM)
SMEM = pl.BlockSpec(memory_space=pltpu.SMEM)
F32 = jnp.float32
BF16 = jnp.bfloat16


def remote(source, target, send, receive, peer):
    return pltpu.make_async_remote_copy(
        src_ref=source,
        dst_ref=target,
        send_sem=send,
        recv_sem=receive,
        device_id=peer,
        device_id_type=MESH,
    )


def dot(left, right, contract):
    return lax.dot_general(left, right, ((contract[:1], contract[1:]), ((), ())), preferred_element_type=F32)


def split(values, parts):
    pieces = []
    for _ in range(parts):
        piece = values.astype(BF16)
        pieces.append(piece)
        values = values - piece.astype(F32)
    return pieces


def place_taps(hi_lo, b, mirrored, hi_at, lo_at):
    rows = hi_lo.shape[0]
    count = TAPS * TAPS
    row = lax.broadcasted_iota(jnp.int32, (rows, LANES), 0)
    lane = lax.broadcasted_iota(jnp.int32, (rows, LANES), 1)
    low = row >= count
    tap = jnp.where(low, row - count, row)
    a, column = lax.div(tap, TAPS), lax.rem(tap, TAPS)
    if mirrored:
        a, column = TAPS - 1 - a, TAPS - 1 - column
    at = jnp.where(low, lo_at, hi_at) + a
    places = jnp.where((column == b) & (lane == at), 1.0, 0.0).astype(BF16)
    return dot(hi_lo, places, (0, 0))


def banded(taps_ref, c, depth):
    parts = []
    for b in range(TAPS):
        part = jnp.broadcast_to(taps_ref[b, pl.ds(c, 1), :], (HALF, LANES))
        parts.append(pltpu.roll(part, 0, 1, stride=1, stride_axis=0))
    return jnp.concatenate(parts, axis=0).astype(BF16)[:, :depth]


def gather_columns(stacked, across):
    lane = lax.broadcasted_iota(jnp.int32, (2 * HALF, across), 1)

    def part(b):
        rows = stacked[b * HALF : (b + 1) * HALF]
        return jnp.concatenate([rows[:, :across], rows[:, across:]], axis=0)

    def leftward(cells):
        return jnp.where(lane < across - 1, pltpu.roll(cells, across - 1, 1), 0.0)

    def rightward(cells):
        return jnp.where(lane > 0, pltpu.roll(cells, 1, 1), 0.0)

    left = part(4) + leftward(part(5) + leftward(part(6)))
    right = part(2) + rightward(part(1) + rightward(part(0)))
    return part(3) + leftward(left) + rightward(right)


def windows(image_ref, halo_ref, c):
    image = image_ref[0, c]
    spare = jnp.zeros((HALF - EDGE, image.shape[1]), F32)
    above = jnp.concatenate([spare, halo_ref[0, c].astype(F32)], axis=0).astype(BF16)
    below = jnp.concatenate([halo_ref[1, c].astype(F32), spare], axis=0).astype(BF16)
    top, bottom = image[:HALF], image[HALF:]
    return [
        jnp.concatenate(pair, axis=1) for pair in ((above, top), (top, bottom), (bottom, below))
    ]


def block_kernel(
    slides, count, share, order_ref, tissue_ref, image_ref, tile_ref, taps_in, channel_ref,
    up_ref, up_bias_ref, down_ref,
    embed_out, grad_out, up_out, down_out, kernel_out,
    fore_taps, back_taps, halo_out, halo_in, tiles_in, held, sums, hidden_sum, slope_gain,
    up_total, cotangent, scaled_mask, columns, bias, edge_out, edge_in, crossed,
    part, near, half, far, whole_sum, kpart, knear, khalf, kfar, kwhole,
    halo_sem, tile_sem, edge_sem, sum_sem, ksum_sem,
):
    slide, me = lax.axis_index("slide"), lax.axis_index("rows")
    channels, height, across = image_ref.shape[1:]
    hidden_units = up_ref.shape[1]
    tiles_here = across // TILE
    across_peers = [(lax.rem(slide + k, slides), me) for k in range(1, slides)]
    along_peers = [(slide, lax.rem(me + k, count)) for k in range(1, count)]
    up_peer, down_peer = along_peers[-1], along_peers[0]
    has_up, has_down = me > 0, me < count - 1

    def edges(out, into, sem):
        return (
            remote(out.at[0], into.at[0], sem.at[0], sem.at[2], down_peer),
            remote(out.at[1], into.at[1], sem.at[1], sem.at[3], up_peer),
        )

    def start_edges(pair):
        pl.when(has_down)(pair[0].start)
        pl.when(has_up)(pair[1].start)

    def finish_edges(pair):
        pl.when(has_down)(pair[0].wait_send)
        pl.when(has_up)(pair[1].wait_send)
        pl.when(has_up)(pair[0].wait_recv)
        pl.when(has_down)(pair[1].wait_recv)

    def pack_edges(c, carry):
        halo_out[0, c] = image_ref[0, c, height - EDGE :, :]
        halo_out[1, c] = image_ref[0, c, :EDGE, :]
        return carry

    barrier = pltpu.get_barrier_semaphore()
    for peer in across_peers + along_peers:
        pl.semaphore_signal(barrier, inc=1, device_id=peer, device_id_type=MESH)
    lax.fori_loop(0, channels, pack_edges, 0, unroll=8)

    @pl.when(jnp.logical_not(has_up))
    def _():
        halo_in[0] = jnp.zeros(halo_in.shape[1:], BF16)
        edge_in[0] = jnp.zeros(edge_in.shape[1:], BF16)

    @pl.when(jnp.logical_not(has_down))
    def _():
        halo_in[1] = jnp.zeros(halo_in.shape[1:], BF16)
        edge_in[1] = jnp.zeros(edge_in.shape[1:], BF16)

    pl.semaphore_wait(barrier, slides + count - 2)
    halo_copies = edges(halo_out, halo_in, halo_sem)
    start_edges(halo_copies)
    tile_copies = [
        remote(tile_ref.at[0], tiles_in.at[me], tile_sem.at[0, k], tile_sem.at[1, k], peer)
        for k, peer in enumerate(along_peers)
    ]
    for copy in tile_copies:
        copy.start()
    tiles_in[me] = tile_ref[0]

    hi_lo = jnp.concatenate([p.astype(F32) for p in split(taps_in[...], 2)], axis=0).astype(BF16)
    for b in range(TAPS):
        fore_taps[b] = place_taps(hi_lo, b, False, HALF - PAD, 4 * HALF - PAD)
        back_taps[b] = place_taps(hi_lo, b, True, 0, HALF + 8)

    turned = jnp.transpose(channel_ref[...])
    for k in range(columns.shape[0]):
        columns[k] = jnp.broadcast_to(turned[:, k : k + 1], (channels, across))
    turned = jnp.transpose(up_bias_ref[...])
    for k in range(hidden_units // LANES):
        bias[k * LANES : (k + 1) * LANES] = jnp.broadcast_to(turned[:, k : k + 1], (LANES, across))
    conv_bias, gain, norm_bias, down_bias, scale = [columns.at[k] for k in range(5)]
    lane = lax.broadcasted_iota(jnp.int32, (1, across), 1)
    mask = jnp.zeros((1, across), F32)
    wanted = jnp.zeros((1, across), jnp.int32)
    for t in range(tiles_here):
        here = lax.div(lane, TILE) == t
        mask = jnp.where(here, tissue_ref[0, 0, t].astype(F32), mask)
        wanted = jnp.where(here, order_ref[0, me * tiles_here + t], wanted)
    scaled_mask[...] = scale[...] * mask
    up_total[...] = jnp.zeros_like(up_total)
    hidden_sum[...] = jnp.zeros_like(hidden_sum)
    held[(height + 2 * PAD) * channels :, :] = jnp.zeros((2 * channels, across), F32)

    for copy in tile_copies:
        copy.wait()
    tiles = jnp.concatenate([tiles_in[k].astype(F32) for k in range(count)], axis=0).astype(BF16)
    chosen = lax.broadcasted_iota(jnp.int32, (tiles.shape[0], across), 0) == wanted
    cotangent[...] = dot(tiles, jnp.where(chosen, 1.0, 0.0).astype(BF16), (0, 0))
    grad_branch = (scaled_mask[...] * cotangent[...]).astype(BF16)
    slope_gain[...] = dot(down_ref[...], grad_branch, (0, 0))

    finish_edges(halo_copies)

    fore_depth = 6 * HALF
    ones = jnp.where(
        (lax.broadcasted_iota(jnp.int32, (HALF, fore_depth), 1) >= HALF)
        & (lax.broadcasted_iota(jnp.int32, (HALF, fore_depth), 1) < 3 * HALF),
        1.0,
        0.0,
    ).astype(BF16)

    def conv_channel(c, carry):
        pieces = windows(image_ref, halo_in, c)
        left = jnp.concatenate([banded(fore_taps, c, fore_depth), ones], axis=0)
        stacked = dot(left, jnp.concatenate(pieces + pieces, axis=0), (1, 0))
        held[pl.ds(PAD * channels + c, height, stride=channels), :] = gather_columns(stacked, across)
        sums[pl.ds(c, 1), :] = stacked[TAPS * HALF : TAPS * HALF + 1, :across]
        return carry

    lax.fori_loop(0, channels, conv_channel, 0, unroll=8)

    blocks = height // ROWS
    edge_copies = edges(edge_out, edge_in, edge_sem)

    def pixels(step, carry):
        block = jnp.where(step == 0, 0, jnp.where(step == 1, blocks - 1, step - 1))

        def start_of(r):
            return pl.multiple_of((block * ROWS + r + PAD) * channels, 8)

        def wide(ref):
            return jnp.concatenate([ref[...]] * ROWS, axis=1)

        conv = jnp.concatenate([held[pl.ds(start_of(r), channels), :] for r in range(ROWS)], axis=1)
        conv = conv + wide(conv_bias)
        average = jnp.mean(conv, axis=0, keepdims=True)
        centered = conv - average
        variance = jnp.mean(centered * centered, axis=0, keepdims=True)
        reciprocal = lax.rsqrt(variance + 1e-06)
        standard = centered * reciprocal
        normed = (standard * wide(gain) + wide(norm_bias)).astype(BF16)
        act = dot(up_ref[...], normed, (0, 0)) + wide(bias)
        cumulative = 0.5 + 0.5 * lax.erf(act * 0.7071067811865476)
        hidden = (act * cumulative).astype(BF16).astype(F32)
        total = hidden_sum[...]
        for r in range(ROWS):
            total = total + hidden[:, r * across : (r + 1) * across]
        hidden_sum[...] = total
        density = jnp.exp(-0.5 * act * act) * 0.3989422804014327
        slope = cumulative + act * density
        grad_act = (wide(slope_gain) * slope).astype(BF16)
        grad_normed = dot(up_ref[...], grad_act, (1, 0))
        up_total[...] += dot(normed, grad_act, (1, 1))
        grad_standard = grad_normed * wide(gain)
        first = jnp.mean(grad_standard, axis=0, keepdims=True)
        second = jnp.mean(grad_standard * standard, axis=0, keepdims=True)
        grad_conv = reciprocal * (grad_standard - first - standard * second)
        for r in range(ROWS):
            held[pl.ds(start_of(r), channels), :] = grad_conv[:, r * across : (r + 1) * across]

        @pl.when(step == 1)
        def _():
            for r in range(PAD):
                low = (height + r) * channels
                edge_out[0, r] = held[low : low + channels, :].astype(BF16)
                low = (PAD + r) * channels
                edge_out[1, r] = held[low : low + channels, :].astype(BF16)
            start_edges(edge_copies)

        return carry

    lax.fori_loop(0, blocks, pixels, 0)

    loss_norm = 1.0 / math.sqrt(slides * count * height * across)
    total_parts = split(hidden_sum[...], 2)
    branch = jnp.zeros((channels, across), F32)
    down = jnp.zeros((channels, hidden_units), F32)
    grad_branch = (scaled_mask[...] * cotangent[...]).astype(BF16)
    for piece in total_parts:
        branch += dot(down_ref[...], piece, (1, 0))
        down += dot(grad_branch, piece, (1, 1))
    embed = sums[...] + scaled_mask[...] * (branch + height * down_bias[...])
    tile_of = lax.div(lax.broadcasted_iota(jnp.int32, (tiles_here, across), 1), TILE)
    picks = jnp.where(
        tile_of == lax.broadcasted_iota(jnp.int32, (tiles_here, across), 0), 1.0, 0.0
    ).astype(BF16)
    embedded = jnp.zeros((tiles_here, channels), F32)
    for piece in split(embed, 3):
        embedded += dot(picks, piece, (1, 1))
    embed_out[0] = embedded * (1.0 / (height * TILE))

    groups = hidden_units // LANES
    pieces = channels // HALF

    def slot_of(index):
        shard, offset = divmod(index * HALF, share)
        return shard // count, shard % count, offset

    used = 2 * groups * pieces
    for index in range(slides * count * share // HALF):
        s, r, offset = slot_of(index)
        if index >= used:
            part[s, r, offset : offset + HALF, :] = jnp.zeros((HALF, LANES), BF16)
            continue
        group, piece = divmod(index, pieces)
        low = piece * HALF
        if group < groups:
            values = up_total[low : low + HALF, group * LANES : (group + 1) * LANES]
        else:
            at = (group - groups) * LANES
            values = down[low : low + HALF, at : at + LANES]
        part[s, r, offset : offset + HALF, :] = (values * loss_norm).astype(BF16)

    def sum_slides(part_ref, near_ref, sem):
        return [
            remote(part_ref.at[peer[0]], near_ref.at[k], sem.at[0, k], sem.at[1, k], peer)
            for k, peer in enumerate(across_peers)
        ]

    def sum_rows(half_ref, far_ref, sem):
        return [
            remote(half_ref.at[peer[1]], far_ref.at[k], sem.at[2, k], sem.at[3, k], peer)
            for k, peer in enumerate(along_peers)
        ]

    def start(copies):
        for copy in copies:
            copy.start()

    def finish(copies):
        for copy in copies:
            copy.wait()

    first = sum_slides(part, near, sum_sem)
    start(first)

    band_row = lax.broadcasted_iota(jnp.int32, (2 * HALF, LANES), 0) + 8
    band_lane = lax.broadcasted_iota(jnp.int32, (2 * HALF, LANES), 1)
    tap = band_row - (HALF - PAD) - lax.rem(band_lane, HALF)
    in_band = (tap >= 0) & (tap < TAPS) & (band_lane < TAPS * HALF)
    fold_row = lax.broadcasted_iota(jnp.int32, (8, LANES), 0)
    row_lane = lax.broadcasted_iota(jnp.int32, (height, across), 1)

    def cross_channel(c, carry):
        grad = held[pl.ds(PAD * channels + c, height, stride=channels), :].astype(BF16)
        rows = []
        for b in range(TAPS):
            s = b - PAD
            moved = grad
            if s:
                moved = pltpu.roll(grad, s % across, 1)
                inside = row_lane >= s if s > 0 else row_lane < across + s
                moved = jnp.where(inside, moved, jnp.zeros((), BF16))
            rows.append(jnp.concatenate([moved[:HALF], moved[HALF:]], axis=1))
        rows.append(jnp.zeros((HALF, 2 * across), BF16))
        image = jnp.concatenate(windows(image_ref, halo_in, c), axis=0)
        cross = dot(image, jnp.concatenate(rows, axis=0), (1, 1))[8 : 8 + 2 * HALF]
        cross = jnp.where(in_band, cross, 0.0)
        total = cross[:8]
        for low in range(8, 2 * HALF, 8):
            total = total + pltpu.roll(cross[low : low + 8], LANES - low, 1)
        for bit in (4, 2, 1):
            moves = lax.rem(lax.div(fold_row, bit), 2) == 1
            total = jnp.where(moves, pltpu.roll(total, LANES - bit, 1), total)
        crossed[pl.ds(pl.multiple_of(c * 8, 8), 8), :] = total
        return carry

    lax.fori_loop(0, channels, cross_channel, 0, unroll=8)

    kernel_term = crossed[pl.ds(0, channels, stride=8), :]
    for k in range(1, 8):
        kernel_term = kernel_term + crossed[pl.ds(k, channels, stride=8), :]
    kernel_term = kernel_term * loss_norm
    kpart[...] = jnp.zeros_like(kpart)
    step_rows = channels // count
    for k in range(count):
        low = k * step_rows
        kpart[k, :step_rows, :] = kernel_term[low : low + step_rows].astype(BF16)
    kfirst = [
        remote(kpart, knear.at[k], ksum_sem.at[0, k], ksum_sem.at[1, k], peer)
        for k, peer in enumerate(across_peers)
    ]
    start(kfirst)

    finish(first)
    for r in range(count):
        total = part[slide, r].astype(F32)
        for k in range(slides - 1):
            total = total + near[k, r].astype(F32)
        half[r] = total.astype(BF16)
    second = sum_rows(half, far, sum_sem)
    start(second)

    finish_edges(edge_copies)
    for r in range(PAD):
        held[r * channels : (r + 1) * channels, :] = edge_in[0, r].astype(F32)
        low = (PAD + height + r) * channels
        held[low : low + channels, :] = edge_in[1, r].astype(F32)

    def back_channel(c, carry):
        grad = held[pl.ds(c, height + 8, stride=channels), :]
        pair = jnp.concatenate([grad[: HALF + 8], grad[HALF:]], axis=1)
        right = jnp.concatenate([pair, pair], axis=0).astype(BF16)
        stacked = dot(banded(back_taps, c, right.shape[0]), right, (1, 0))
        conv = gather_columns(stacked, across)
        grad_out[0, c] = (conv + cotangent[pl.ds(c, 1), :]).astype(BF16)
        return carry

    third_of = channels // 3
    lax.fori_loop(0, third_of, back_channel, 0, unroll=8)

    finish(kfirst)
    for r in range(count):
        total = kpart[r].astype(F32)
        for k in range(slides - 1):
            total = total + knear[k, r].astype(F32)
        khalf[r] = total.astype(BF16)
    ksecond = sum_rows(khalf, kfar, ksum_sem)
    start(ksecond)
    finish(second)
    total = half[me].astype(F32)
    for k in range(count - 1):
        total = total + far[k].astype(F32)
    whole_sum[slide, me] = total.astype(BF16)
    third = [
        remote(whole_sum.at[slide, me], whole_sum.at[slide, me], sum_sem.at[4, k], sum_sem.at[5, k], peer)
        for k, peer in enumerate(along_peers)
    ]
    start(third)

    lax.fori_loop(third_of, 2 * third_of, back_channel, 0, unroll=8)

    finish(ksecond)
    total = khalf[me].astype(F32)
    for k in range(count - 1):
        total = total + kfar[k].astype(F32)
    kwhole[me] = total.astype(BF16)
    kthird = [
        remote(kwhole.at[me], kwhole.at[me], ksum_sem.at[4, k], ksum_sem.at[5, k], peer)
        for k, peer in enumerate(along_peers)
    ]
    start(kthird)
    finish(third)
    fourth = [
        remote(whole_sum.at[slide], whole_sum.at[slide], sum_sem.at[6, k], sum_sem.at[7, k], peer)
        for k, peer in enumerate(across_peers)
    ]
    start(fourth)

    lax.fori_loop(2 * third_of, channels, back_channel, 0, unroll=8)

    finish(kthird)
    rows = jnp.concatenate([kwhole[k, :step_rows, :].astype(F32) for k in range(count)], axis=0)
    tap = lax.broadcasted_iota(jnp.int32, (TAPS * TAPS, LANES), 0)
    at = HALF * lax.rem(tap, TAPS) - lax.div(tap, TAPS) - (HALF - PAD) + 8 + LANES
    at = lax.rem(at, LANES) == lax.broadcasted_iota(jnp.int32, (TAPS * TAPS, LANES), 1)
    kernel_out[...] = dot(jnp.where(at, 1.0, 0.0).astype(BF16), rows.astype(BF16), (1, 1))
    finish(fourth)
    for index in range(used):
        s, r, offset = slot_of(index)
        group, piece = divmod(index, pieces)
        low = piece * HALF
        values = whole_sum[s, r, offset : offset + HALF, :].astype(F32)
        target = up_out if group < groups else down_out
        at = group % groups * LANES
        target[low : low + HALF, at : at + LANES] = values


def on_device(
    features,
    depth_kernel,
    depth_bias,
    norm_gain,
    norm_bias,
    up_weight,
    up_bias,
    down_weight,
    down_bias,
    layer_scale,
    tissue,
    aggregator_order,
    tile_cotangent,
):
    channels, height, across = features.shape[1:]
    hidden_units = up_weight.shape[1]
    tiles_here = across // TILE
    slides, count = lax.axis_size("slide"), lax.axis_size("rows")
    entries = 2 * channels * hidden_units // LANES
    share = HALF * pl.cdiv(entries, HALF * slides * count)
    kshare = HALF * pl.cdiv(channels // count, HALF)
    span = (slides, count, share, LANES)
    kspan = (count, kshare, LANES)
    most = max(slides, count) - 1
    dma = pltpu.SemaphoreType.DMA
    embedding, input_grad, grad_up, grad_down, grad_kernel = pl.pallas_call(
        functools.partial(block_kernel, slides, count, share),
        out_shape=(
            jax.ShapeDtypeStruct((1, tiles_here, channels), F32),
            jax.ShapeDtypeStruct(features.shape, BF16),
            jax.ShapeDtypeStruct((channels, hidden_units), F32),
            jax.ShapeDtypeStruct((channels, hidden_units), F32),
            jax.ShapeDtypeStruct((TAPS * TAPS, channels), F32),
        ),
        in_specs=[SMEM, SMEM] + [VMEM] * 7,
        out_specs=(VMEM,) * 5,
        scratch_shapes=[
            pltpu.VMEM((TAPS, channels, LANES), F32),
            pltpu.VMEM((TAPS, channels, LANES), F32),
            pltpu.VMEM((2, channels, EDGE, across), BF16),
            pltpu.VMEM((2, channels, EDGE, across), BF16),
            pltpu.VMEM((count, tiles_here, channels), BF16),
            pltpu.VMEM(((height + 8) * channels, across), F32),
            pltpu.VMEM((channels, across), F32),
            pltpu.VMEM((hidden_units, across), F32),
            pltpu.VMEM((hidden_units, across), F32),
            pltpu.VMEM((channels, hidden_units), F32),
            pltpu.VMEM((channels, across), F32),
            pltpu.VMEM((channels, across), F32),
            pltpu.VMEM((5, channels, across), F32),
            pltpu.VMEM((hidden_units, across), F32),
            pltpu.VMEM((2, PAD, channels, across), BF16),
            pltpu.VMEM((2, PAD, channels, across), BF16),
            pltpu.VMEM((channels * 8, LANES), F32),
            pltpu.VMEM(span, BF16),
            pltpu.VMEM((slides - 1,) + span[1:], BF16),
            pltpu.VMEM(span[1:], BF16),
            pltpu.VMEM((count - 1,) + span[2:], BF16),
            pltpu.VMEM(span, BF16),
            pltpu.VMEM(kspan, BF16),
            pltpu.VMEM((slides - 1,) + kspan, BF16),
            pltpu.VMEM(kspan, BF16),
            pltpu.VMEM((count - 1,) + kspan[1:], BF16),
            pltpu.VMEM(kspan, BF16),
            dma((4,)),
            dma((2, most)),
            dma((4,)),
            dma((8, most)),
            dma((6, most)),
        ],
        compiler_params=pltpu.CompilerParams(
            collective_id=0, has_side_effects=True, vmem_limit_bytes=56 * 1024 * 1024
        ),
        name="block",
    )(
        aggregator_order,
        tissue,
        features,
        tile_cotangent,
        depth_kernel.T,
        jnp.stack([depth_bias, norm_gain, norm_bias, down_bias, layer_scale] + [layer_scale] * 3),
        up_weight,
        up_bias.reshape(-1, LANES),
        down_weight.T,
    )
    return embedding, input_grad, grad_up, grad_down.T, grad_kernel.T


def solution(mesh):
    return jax.shard_map(
        on_device,
        mesh=mesh,
        in_specs=(
            P("slide", None, "rows", None),
            P(),
            P(),
            P(),
            P(),
            P(),
            P(),
            P(),
            P(),
            P(),
            P("slide", "rows", None),
            P("slide", None),
            P("slide", "rows", None),
        ),
        out_specs=(P("slide", "rows", None), P("slide", None, "rows", None), P(), P(), P()),
        check_vma=False,
    )
```

```python
import functools
import math

import jax
import jax.numpy as jnp
from jax import lax
from jax.experimental import pallas as pl
from jax.experimental.pallas import tpu as pltpu
from jax.sharding import PartitionSpec as P

TILE = 32
ROWS = 4
HALF = 16
TAPS = 7
PAD = 3
EDGE = 4
OUTER = 8
LANES = 128
MESH = pl.DeviceIdType.MESH
VMEM = pl.BlockSpec(memory_space=pltpu.VMEM)
SMEM = pl.BlockSpec(memory_space=pltpu.SMEM)
F32 = jnp.float32
BF16 = jnp.bfloat16


def remote(source, target, send, receive, peer):
    return pltpu.make_async_remote_copy(
        src_ref=source,
        dst_ref=target,
        send_sem=send,
        recv_sem=receive,
        device_id=peer,
        device_id_type=MESH,
    )


def dot(left, right, contract):
    return lax.dot_general(left, right, ((contract[:1], contract[1:]), ((), ())), preferred_element_type=F32)


def split(values, parts):
    pieces = []
    for _ in range(parts):
        piece = values.astype(BF16)
        pieces.append(piece)
        values = values - piece.astype(F32)
    return pieces


def place_taps(hi_lo, b, mirrored, hi_at, lo_at):
    rows = hi_lo.shape[0]
    count = TAPS * TAPS
    row = lax.broadcasted_iota(jnp.int32, (rows, LANES), 0)
    lane = lax.broadcasted_iota(jnp.int32, (rows, LANES), 1)
    low = row >= count
    tap = jnp.where(low, row - count, row)
    a, column = lax.div(tap, TAPS), lax.rem(tap, TAPS)
    if mirrored:
        a, column = TAPS - 1 - a, TAPS - 1 - column
    at = jnp.where(low, lo_at, hi_at) + a
    places = jnp.where((column == b) & (lane == at), 1.0, 0.0).astype(BF16)
    return dot(hi_lo, places, (0, 0))


def banded(taps_ref, c, depth):
    parts = []
    for b in range(TAPS):
        part = jnp.broadcast_to(taps_ref[b, pl.ds(c, 1), :], (HALF, LANES))
        parts.append(pltpu.roll(part, 0, 1, stride=1, stride_axis=0))
    return jnp.concatenate(parts, axis=0).astype(BF16)[:, :depth]


def gather_columns(stacked, across):
    lane = lax.broadcasted_iota(jnp.int32, (2 * HALF, across), 1)

    def part(b):
        rows = stacked[b * HALF : (b + 1) * HALF]
        return jnp.concatenate([rows[:, :across], rows[:, across:]], axis=0)

    def leftward(cells):
        return jnp.where(lane < across - 1, pltpu.roll(cells, across - 1, 1), 0.0)

    def rightward(cells):
        return jnp.where(lane > 0, pltpu.roll(cells, 1, 1), 0.0)

    left = part(4) + leftward(part(5) + leftward(part(6)))
    right = part(2) + rightward(part(1) + rightward(part(0)))
    return part(3) + leftward(left) + rightward(right)


def windows(image_ref, halo_ref, c):
    image = image_ref[0, c]
    spare = jnp.zeros((HALF - EDGE, image.shape[1]), F32)
    above = jnp.concatenate([spare, halo_ref[0, c].astype(F32)], axis=0).astype(BF16)
    below = jnp.concatenate([halo_ref[1, c].astype(F32), spare], axis=0).astype(BF16)
    top, bottom = image[:HALF], image[HALF:]
    return [
        jnp.concatenate(pair, axis=1) for pair in ((above, top), (top, bottom), (bottom, below))
    ]


def slots(slides, count, share, channels, units):
    groups, pieces = units // LANES, channels // OUTER
    found = []
    for index in range(slides * count * share // OUTER):
        shard, offset = divmod(index * OUTER, share)
        group, piece = divmod(index, pieces)
        side, column = divmod(group, groups)
        if side > 1:
            side = None
        found.append((shard // count, shard % count, offset, side, piece * OUTER, column * LANES))
    return found


def block_kernel(
    slides, count, share, order_ref, tissue_ref, image_ref, tile_ref, taps_in, channel_ref,
    up_ref, up_bias_ref, down_ref,
    embed_out, grad_out, whole_sum, kernel_out,
    fore_taps, back_taps, halo_out, halo_in, tiles_in, held, sums, hidden_sum, slope_gain,
    up_total, cotangent, scaled_mask, columns, bias, edge_out, edge_in, crossed,
    grad_sum, part, near, half, far, kpart, knear, khalf, kfar, kwhole,
    halo_sem, tile_sem, edge_sem, sum_sem, ksum_sem,
):
    slide, me = lax.axis_index("slide"), lax.axis_index("rows")
    channels, height, across = image_ref.shape[1:]
    hidden_units = up_ref.shape[1]
    tiles_here = across // TILE
    across_peers = [(lax.rem(slide + k, slides), me) for k in range(1, slides)]
    along_peers = [(slide, lax.rem(me + k, count)) for k in range(1, count)]
    up_peer, down_peer = along_peers[-1], along_peers[0]
    has_up, has_down = me > 0, me < count - 1

    def edges(out, into, sem):
        return (
            remote(out.at[0], into.at[0], sem.at[0], sem.at[2], down_peer),
            remote(out.at[1], into.at[1], sem.at[1], sem.at[3], up_peer),
        )

    def start_edges(pair):
        pl.when(has_down)(pair[0].start)
        pl.when(has_up)(pair[1].start)

    def finish_edges(pair):
        pl.when(has_down)(pair[0].wait_send)
        pl.when(has_up)(pair[1].wait_send)
        pl.when(has_up)(pair[0].wait_recv)
        pl.when(has_down)(pair[1].wait_recv)

    def pack_edges(c, carry):
        halo_out[0, c] = image_ref[0, c, height - EDGE :, :]
        halo_out[1, c] = image_ref[0, c, :EDGE, :]
        return carry

    barrier = pltpu.get_barrier_semaphore()
    for peer in across_peers + along_peers:
        pl.semaphore_signal(barrier, inc=1, device_id=peer, device_id_type=MESH)
    lax.fori_loop(0, channels, pack_edges, 0, unroll=8)

    @pl.when(jnp.logical_not(has_up))
    def _():
        halo_in[0] = jnp.zeros(halo_in.shape[1:], BF16)
        edge_in[0] = jnp.zeros(edge_in.shape[1:], BF16)

    @pl.when(jnp.logical_not(has_down))
    def _():
        halo_in[1] = jnp.zeros(halo_in.shape[1:], BF16)
        edge_in[1] = jnp.zeros(edge_in.shape[1:], BF16)

    pl.semaphore_wait(barrier, slides + count - 2)
    halo_copies = edges(halo_out, halo_in, halo_sem)
    start_edges(halo_copies)
    tile_copies = [
        remote(tile_ref.at[0], tiles_in.at[me], tile_sem.at[0, k], tile_sem.at[1, k], peer)
        for k, peer in enumerate(along_peers)
    ]
    for copy in tile_copies:
        copy.start()
    tiles_in[me] = tile_ref[0]

    hi_lo = jnp.concatenate([p.astype(F32) for p in split(taps_in[...], 2)], axis=0).astype(BF16)
    for b in range(TAPS):
        fore_taps[b] = place_taps(hi_lo, b, False, HALF - PAD, 4 * HALF - PAD)
        back_taps[b] = place_taps(hi_lo, b, True, 0, HALF + 8)

    turned = jnp.transpose(channel_ref[...])
    for k in range(columns.shape[0]):
        columns[k] = jnp.broadcast_to(turned[:, k : k + 1], (channels, across))
    turned = jnp.transpose(up_bias_ref[...])
    for k in range(hidden_units // LANES):
        bias[k * LANES : (k + 1) * LANES] = jnp.broadcast_to(turned[:, k : k + 1], (LANES, across))
    conv_bias, gain, norm_bias, down_bias, scale = [columns.at[k] for k in range(5)]
    lane = lax.broadcasted_iota(jnp.int32, (1, across), 1)
    mask = jnp.zeros((1, across), F32)
    wanted = jnp.zeros((1, across), jnp.int32)
    for t in range(tiles_here):
        here = lax.div(lane, TILE) == t
        mask = jnp.where(here, tissue_ref[0, 0, t].astype(F32), mask)
        wanted = jnp.where(here, order_ref[0, me * tiles_here + t], wanted)
    scaled_mask[...] = scale[...] * mask
    up_total[...] = jnp.zeros_like(up_total)
    hidden_sum[...] = jnp.zeros_like(hidden_sum)
    held[(height + 2 * PAD) * channels :, :] = jnp.zeros((2 * channels, across), F32)

    for copy in tile_copies:
        copy.wait()
    tiles = jnp.concatenate([tiles_in[k].astype(F32) for k in range(count)], axis=0).astype(BF16)
    chosen = lax.broadcasted_iota(jnp.int32, (tiles.shape[0], across), 0) == wanted
    cotangent[...] = dot(tiles, jnp.where(chosen, 1.0, 0.0).astype(BF16), (0, 0))
    grad_branch = (scaled_mask[...] * cotangent[...]).astype(BF16)
    slope_gain[...] = dot(down_ref[...], grad_branch, (0, 0))

    finish_edges(halo_copies)

    fore_depth = 6 * HALF
    ones = jnp.where(
        (lax.broadcasted_iota(jnp.int32, (HALF, fore_depth), 1) >= HALF)
        & (lax.broadcasted_iota(jnp.int32, (HALF, fore_depth), 1) < 3 * HALF),
        1.0,
        0.0,
    ).astype(BF16)

    def conv_channel(c, carry):
        pieces = windows(image_ref, halo_in, c)
        left = jnp.concatenate([banded(fore_taps, c, fore_depth), ones], axis=0)
        stacked = dot(left, jnp.concatenate(pieces + pieces, axis=0), (1, 0))
        held[pl.ds(PAD * channels + c, height, stride=channels), :] = gather_columns(stacked, across)
        sums[pl.ds(c, 1), :] = stacked[TAPS * HALF : TAPS * HALF + 1, :across]
        return carry

    lax.fori_loop(0, channels, conv_channel, 0, unroll=16)

    blocks = height // ROWS
    edge_copies = edges(edge_out, edge_in, edge_sem)

    units = hidden_units // 2
    loss_norm = 1.0 / math.sqrt(slides * count * height * across)

    def start(copies):
        for copy in copies:
            copy.start()

    def finish(copies):
        for copy in copies:
            copy.wait()

    def add_parts(own, others, number):
        total = own.astype(F32)
        for k in range(number):
            total = total + others(k).astype(F32)
        return total.astype(BF16)

    def to_slides(source, target, sem, pair, place):
        return [
            remote(
                source.at[peer[0]] if place is None else source.at[place],
                target.at[k] if place is None else target.at[place],
                sem.at[pair, k], sem.at[pair + 1, k], peer,
            )
            for k, peer in enumerate(across_peers)
        ]

    def to_rows(source, target, sem, pair, place):
        return [
            remote(
                source.at[peer[1]] if place is None else source.at[place],
                target.at[k] if place is None else target.at[place],
                sem.at[pair, k], sem.at[pair + 1, k], peer,
            )
            for k, peer in enumerate(along_peers)
        ]

    stages = []
    for h in range(2):
        mine = whole_sum.at[h, slide]
        stages.append(
            [
                to_slides(part.at[h], near.at[h], sum_sem.at[h], 0, None),
                to_rows(half.at[h], far.at[h], sum_sem.at[h], 2, None),
                to_rows(mine, mine, sum_sem.at[h], 4, me),
                to_slides(whole_sum.at[h], whole_sum.at[h], sum_sem.at[h], 6, slide),
            ]
        )

    def add_slides(h):
        finish(stages[h][0])
        for r in range(count):
            half[h, r] = add_parts(part[h, slide, r], lambda k: near[h, k, r], slides - 1)
        start(stages[h][1])

    def add_rows(h):
        finish(stages[h][1])
        whole_sum[h, slide, me] = add_parts(half[h, me], lambda k: far[h, k], count - 1)
        start(stages[h][2])

    def pass_on(h):
        finish(stages[h][2])
        start(stages[h][3])

    def wide(cells):
        return jnp.concatenate([cells] * ROWS, axis=1)

    def pixels(h, step, carry):
        block = jnp.where(step == 0, 0, jnp.where(step == 1, blocks - 1, step - 1))
        mine = slice(h * units, (h + 1) * units)

        def start_of(r):
            return pl.multiple_of((block * ROWS + r + PAD) * channels, 8)

        conv = jnp.concatenate([held[pl.ds(start_of(r), channels), :] for r in range(ROWS)], axis=1)
        conv = conv + wide(conv_bias[...])
        average = jnp.mean(conv, axis=0, keepdims=True)
        centered = conv - average
        variance = jnp.mean(centered * centered, axis=0, keepdims=True)
        reciprocal = lax.rsqrt(variance + 1e-06)
        standard = centered * reciprocal
        normed = (standard * wide(gain[...]) + wide(norm_bias[...])).astype(BF16)
        act = dot(up_ref[:, mine], normed, (0, 0)) + wide(bias[mine])
        cumulative = 0.5 + 0.5 * lax.erf(act * 0.7071067811865476)
        hidden = (act * cumulative).astype(BF16).astype(F32)
        total = hidden_sum[mine]
        for r in range(ROWS):
            total = total + hidden[:, r * across : (r + 1) * across]
        hidden_sum[mine] = total
        density = jnp.exp(-0.5 * act * act) * 0.3989422804014327
        slope = cumulative + act * density
        grad_act = (wide(slope_gain[mine]) * slope).astype(BF16)
        grad_normed = dot(up_ref[:, mine], grad_act, (1, 0))
        up_total[:, mine] += dot(normed, grad_act, (1, 1))
        if h == 0:
            grad_sum[block] = grad_normed
            return carry
        grad_standard = (grad_sum[block] + grad_normed) * wide(gain[...])
        first = jnp.mean(grad_standard, axis=0, keepdims=True)
        second = jnp.mean(grad_standard * standard, axis=0, keepdims=True)
        grad_conv = reciprocal * (grad_standard - first - standard * second)
        for r in range(ROWS):
            held[pl.ds(start_of(r), channels), :] = grad_conv[:, r * across : (r + 1) * across]

        @pl.when(step == 1)
        def _():
            for r in range(PAD):
                low = (height + r) * channels
                edge_out[0, r] = held[low : low + channels, :].astype(BF16)
                low = (PAD + r) * channels
                edge_out[1, r] = held[low : low + channels, :].astype(BF16)
            start_edges(edge_copies)

        @pl.when(step == blocks // 2)
        def _():
            add_slides(0)

        return carry

    grad_branch = (scaled_mask[...] * cotangent[...]).astype(BF16)
    branch = jnp.zeros((channels, across), F32)
    for h in range(2):
        lax.fori_loop(0, blocks, functools.partial(pixels, h), 0)
        mine = slice(h * units, (h + 1) * units)
        down = jnp.zeros((channels, units), F32)
        for piece in split(hidden_sum[mine], 2):
            branch += dot(down_ref[:, mine], piece, (1, 0))
            down += dot(grad_branch, piece, (1, 1))
        for s, r, offset, side, low, at in slots(slides, count, share, channels, units):
            if side is None:
                values = jnp.zeros((OUTER, LANES), F32)
            elif side == 0:
                values = up_total[low : low + OUTER, h * units + at : h * units + at + LANES]
            else:
                values = down[low : low + OUTER, at : at + LANES]
            part[h, s, r, offset : offset + OUTER, :] = (values * loss_norm).astype(BF16)
        start(stages[h][0])

    add_rows(0)
    embed = sums[...] + scaled_mask[...] * (branch + height * down_bias[...])
    tile_of = lax.div(lax.broadcasted_iota(jnp.int32, (tiles_here, across), 1), TILE)
    picks = jnp.where(
        tile_of == lax.broadcasted_iota(jnp.int32, (tiles_here, across), 0), 1.0, 0.0
    ).astype(BF16)
    embedded = jnp.zeros((tiles_here, channels), F32)
    for piece in split(embed, 3):
        embedded += dot(picks, piece, (1, 1))
    embed_out[0] = embedded * (1.0 / (height * TILE))

    band_row = lax.broadcasted_iota(jnp.int32, (2 * HALF, LANES), 0) + 8
    band_lane = lax.broadcasted_iota(jnp.int32, (2 * HALF, LANES), 1)
    tap = band_row - (HALF - PAD) - lax.rem(band_lane, HALF)
    in_band = (tap >= 0) & (tap < TAPS) & (band_lane < TAPS * HALF)
    fold_row = lax.broadcasted_iota(jnp.int32, (8, LANES), 0)
    row_lane = lax.broadcasted_iota(jnp.int32, (height, across), 1)

    def cross_channel(c, carry):
        grad = held[pl.ds(PAD * channels + c, height, stride=channels), :].astype(BF16)
        rows = []
        for b in range(TAPS):
            s = b - PAD
            moved = grad
            if s:
                moved = pltpu.roll(grad, s % across, 1)
                inside = row_lane >= s if s > 0 else row_lane < across + s
                moved = jnp.where(inside, moved, jnp.zeros((), BF16))
            rows.append(jnp.concatenate([moved[:HALF], moved[HALF:]], axis=1))
        rows.append(jnp.zeros((HALF, 2 * across), BF16))
        image = jnp.concatenate(windows(image_ref, halo_in, c), axis=0)
        cross = dot(image, jnp.concatenate(rows, axis=0), (1, 1))[8 : 8 + 2 * HALF]
        cross = jnp.where(in_band, cross, 0.0)
        total = cross[:8]
        for low in range(8, 2 * HALF, 8):
            total = total + pltpu.roll(cross[low : low + 8], LANES - low, 1)
        for bit in (4, 2, 1):
            moves = lax.rem(lax.div(fold_row, bit), 2) == 1
            total = jnp.where(moves, pltpu.roll(total, LANES - bit, 1), total)
        crossed[pl.ds(pl.multiple_of(c * 8, 8), 8), :] = total
        return carry

    lax.fori_loop(0, channels, cross_channel, 0, unroll=16)

    kernel_term = crossed[pl.ds(0, channels, stride=8), :]
    for k in range(1, 8):
        kernel_term = kernel_term + crossed[pl.ds(k, channels, stride=8), :]
    kernel_term = kernel_term * loss_norm
    kpart[...] = jnp.zeros_like(kpart)
    step_rows = channels // count
    for k in range(count):
        low = k * step_rows
        kpart[k, :step_rows, :] = kernel_term[low : low + step_rows].astype(BF16)
    kstages = [
        [
            remote(kpart, knear.at[k], ksum_sem.at[0, k], ksum_sem.at[1, k], peer)
            for k, peer in enumerate(across_peers)
        ],
        to_rows(khalf, kfar, ksum_sem, 2, None),
        to_rows(kwhole, kwhole, ksum_sem, 4, me),
    ]
    start(kstages[0])
    add_slides(1)
    pass_on(0)

    finish_edges(edge_copies)
    for r in range(PAD):
        held[r * channels : (r + 1) * channels, :] = edge_in[0, r].astype(F32)
        low = (PAD + height + r) * channels
        held[low : low + channels, :] = edge_in[1, r].astype(F32)

    def back_channel(c, carry):
        grad = held[pl.ds(c, height + 8, stride=channels), :]
        pair = jnp.concatenate([grad[: HALF + 8], grad[HALF:]], axis=1)
        right = jnp.concatenate([pair, pair], axis=0).astype(BF16)
        stacked = dot(banded(back_taps, c, right.shape[0]), right, (1, 0))
        conv = gather_columns(stacked, across)
        grad_out[0, c] = (conv + cotangent[pl.ds(c, 1), :]).astype(BF16)
        return carry

    third_of = channels // 3
    lax.fori_loop(0, third_of, back_channel, 0, unroll=8)

    finish(kstages[0])
    for r in range(count):
        khalf[r] = add_parts(kpart[r], lambda k: knear[k, r], slides - 1)
    start(kstages[1])
    add_rows(1)

    lax.fori_loop(third_of, 2 * third_of, back_channel, 0, unroll=8)

    finish(kstages[1])
    kwhole[me] = add_parts(khalf[me], lambda k: kfar[k], count - 1)
    start(kstages[2])
    pass_on(1)

    lax.fori_loop(2 * third_of, channels, back_channel, 0, unroll=8)

    finish(kstages[2])
    rows = jnp.concatenate([kwhole[k, :step_rows, :].astype(F32) for k in range(count)], axis=0)
    tap = lax.broadcasted_iota(jnp.int32, (TAPS * TAPS, LANES), 0)
    at = HALF * lax.rem(tap, TAPS) - lax.div(tap, TAPS) - (HALF - PAD) + 8 + LANES
    at = lax.rem(at, LANES) == lax.broadcasted_iota(jnp.int32, (TAPS * TAPS, LANES), 1)
    kernel_out[...] = dot(jnp.where(at, 1.0, 0.0).astype(BF16), rows.astype(BF16), (1, 1))
    finish(stages[0][3])
    finish(stages[1][3])


def spread_kernel(grad_ref, whole_ref, grad_out, up_out, down_out):
    grad_out[...] = grad_ref[...]
    halves, slides, count, share, _ = whole_ref.shape
    channels, hidden_units = up_out.shape
    units = hidden_units // halves
    for h in range(halves):
        for s, r, offset, side, low, at in slots(slides, count, share, channels, units):
            if side is None:
                continue
            target = (up_out, down_out)[side]
            values = whole_ref[h, s, r, offset : offset + OUTER, :].astype(F32)
            target[low : low + OUTER, h * units + at : h * units + at + LANES] = values


def on_device(
    features,
    depth_kernel,
    depth_bias,
    norm_gain,
    norm_bias,
    up_weight,
    up_bias,
    down_weight,
    down_bias,
    layer_scale,
    tissue,
    aggregator_order,
    tile_cotangent,
):
    channels, height, across = features.shape[1:]
    hidden_units = up_weight.shape[1]
    tiles_here = across // TILE
    slides, count = lax.axis_size("slide"), lax.axis_size("rows")
    entries = channels * hidden_units // LANES
    share = OUTER * pl.cdiv(entries, OUTER * slides * count)
    kshare = HALF * pl.cdiv(channels // count, HALF)
    span = (2, slides, count, share, LANES)
    kspan = (count, kshare, LANES)
    most = max(slides, count) - 1
    dma = pltpu.SemaphoreType.DMA
    embedding, input_grad, whole_sum, grad_kernel = pl.pallas_call(
        functools.partial(block_kernel, slides, count, share),
        out_shape=(
            jax.ShapeDtypeStruct((1, tiles_here, channels), F32),
            jax.ShapeDtypeStruct(features.shape, BF16),
            jax.ShapeDtypeStruct(span, BF16),
            jax.ShapeDtypeStruct((TAPS * TAPS, channels), F32),
        ),
        in_specs=[SMEM, SMEM] + [VMEM] * 7,
        out_specs=(VMEM,) * 4,
        scratch_shapes=[
            pltpu.VMEM((TAPS, channels, LANES), F32),
            pltpu.VMEM((TAPS, channels, LANES), F32),
            pltpu.VMEM((2, channels, EDGE, across), BF16),
            pltpu.VMEM((2, channels, EDGE, across), BF16),
            pltpu.VMEM((count, tiles_here, channels), BF16),
            pltpu.VMEM(((height + 8) * channels, across), F32),
            pltpu.VMEM((channels, across), F32),
            pltpu.VMEM((hidden_units, across), F32),
            pltpu.VMEM((hidden_units, across), F32),
            pltpu.VMEM((channels, hidden_units), F32),
            pltpu.VMEM((channels, across), F32),
            pltpu.VMEM((channels, across), F32),
            pltpu.VMEM((5, channels, across), F32),
            pltpu.VMEM((hidden_units, across), F32),
            pltpu.VMEM((2, PAD, channels, across), BF16),
            pltpu.VMEM((2, PAD, channels, across), BF16),
            pltpu.VMEM((channels * 8, LANES), F32),
            pltpu.VMEM((height // ROWS, channels, ROWS * across), F32),
            pltpu.VMEM(span, BF16),
            pltpu.VMEM((2, slides - 1) + span[2:], BF16),
            pltpu.VMEM((2,) + span[2:], BF16),
            pltpu.VMEM((2, count - 1) + span[3:], BF16),
            pltpu.VMEM(kspan, BF16),
            pltpu.VMEM((slides - 1,) + kspan, BF16),
            pltpu.VMEM(kspan, BF16),
            pltpu.VMEM((count - 1,) + kspan[1:], BF16),
            pltpu.VMEM(kspan, BF16),
            dma((4,)),
            dma((2, most)),
            dma((4,)),
            dma((2, 8, most)),
            dma((6, most)),
        ],
        compiler_params=pltpu.CompilerParams(
            collective_id=0, has_side_effects=True, vmem_limit_bytes=56 * 1024 * 1024
        ),
        name="block",
    )(
        aggregator_order,
        tissue,
        features,
        tile_cotangent,
        depth_kernel.T,
        jnp.stack([depth_bias, norm_gain, norm_bias, down_bias, layer_scale] + [layer_scale] * 3),
        up_weight,
        up_bias.reshape(-1, LANES),
        down_weight.T,
    )
    input_grad, grad_up, grad_down = pl.pallas_call(
        spread_kernel,
        out_shape=(
            jax.ShapeDtypeStruct(features.shape, BF16),
            jax.ShapeDtypeStruct((channels, hidden_units), F32),
            jax.ShapeDtypeStruct((channels, hidden_units), F32),
        ),
        in_specs=[VMEM] * 2,
        out_specs=(VMEM,) * 3,
        name="spread",
    )(input_grad, whole_sum)
    return embedding, input_grad, grad_up, grad_down.T, grad_kernel.T


def solution(mesh):
    return jax.shard_map(
        on_device,
        mesh=mesh,
        in_specs=(
            P("slide", None, "rows", None),
            P(),
            P(),
            P(),
            P(),
            P(),
            P(),
            P(),
            P(),
            P(),
            P("slide", "rows", None),
            P("slide", None),
            P("slide", "rows", None),
        ),
        out_specs=(P("slide", "rows", None), P("slide", None, "rows", None), P(), P(), P()),
        check_vma=False,
    )
```
